32 devices in a mesh: row: 8 (over y, x, core), col: 4 (over z).
Axes of the slice: x: 2, y: 2, z: 4, core: 2. Of those that a mesh axis runs over, the one named last changes fastest.
Arguments:
- in_map: bfloat16 [128, 128, 256], P('row', 'col'), may hold values from -6 to 6
- tile_w: bfloat16 [3, 3, 256, 256], replicated, may hold values from -0.125 to 0.125
- head_w1: bfloat16 [3, 3, 256, 256], replicated, may hold values from -0.125 to 0.125
- head_w2: bfloat16 [3, 3, 256, 256], replicated, may hold values from -0.125 to 0.125
- box_row: int32 [64, 4], P('row', 'col'), may hold values from 0 to 2
- box_col: int32 [64, 4], P('row', 'col'), may hold values from 0 to 18
- box_target: int32 [64, 4], P('row', 'col'), may hold values from -1 to 15, as said below
- head_cot: bfloat16 [32, 4, 14, 14, 256], P('row', 'col'), may hold values from -6 to 6
Outputs:
- grad_map: bfloat16 [128, 128, 256], P('row', 'col')
- grad_w1: float32 [3, 3, 256, 256], replicated
- grad_w2: float32 [3, 3, 256, 256], replicated
The draws below stay inside these ranges and needn't reach their ends.
Inputs may be any that keep to these rules, and one draw needn't show every extreme that they name: `box_target`: within each row r of tiles, every head slot d * 4 + h (d below 4, h below 4) is named by exactly one tile slot, and empty slots hold -1. A tile names at most 2 head slots of one device, so it holds at most 8 boxes; in every row of tiles one tile holds 8 boxes, 2 for each device of the row.
All inputs are finite; a program needn't handle non-finite values.
Results may differ from the reference program's by a relative error of at most 0.012.
Values may be sent and summed in bfloat16 or wider, within the bound.
No kernel may reach another device: no remote copies, remote signals or barrier semaphores. Data moves between devices by JAX's collectives and lax.ppermute only.
A program may use at most 64 MiB of HBM per device.

```python
import math
import jax
import jax.numpy as jnp
from jax import lax

C = 256
BOX = 14
TR = 16
TC = 32
HB = 4
CAP = 2
SLOTS = 8
H = 128
W = 128
N_ROW = 8
N_COL = 4


def draw_box_target(key, part):

    def one_row(row_key):
        keys = jax.random.split(row_key, 5)
        heavy = jax.random.randint(keys[0], (), 0, N_COL).astype(jnp.int32)
        others = jax.random.randint(keys[1], (N_COL, HB - CAP), 0, N_COL - 1).astype(jnp.int32)
        others = others + (others >= heavy).astype(jnp.int32)
        source = jnp.concatenate([jnp.full((N_COL, CAP), heavy, jnp.int32), others], axis=1)
        order = jax.vmap(lambda k: jax.random.permutation(k, HB))(jax.random.split(keys[2], N_COL)).astype(jnp.int32)
        target = jnp.arange(N_COL, dtype=jnp.int32)[:, None] * HB + order
        source = source.reshape(-1)
        target = target.reshape(-1)
        priority = jax.random.permutation(keys[3], N_COL * HB).astype(jnp.int32)
        same_source = source[:, None] == source[None, :]
        ranking = jnp.sum(same_source & (priority[None, :] < priority[:, None]), axis=1).astype(jnp.int32)
        slot_perm = jax.vmap(lambda k: jax.random.permutation(k, SLOTS))(jax.random.split(keys[4], N_COL)).astype(jnp.int32)
        slot_of = slot_perm[source, ranking]
        table = jnp.full((N_COL, SLOTS), -1, jnp.int32).at[source, slot_of].set(target)
        return table.T
    tables = jax.vmap(one_row)(jax.random.split(jax.random.fold_in(key, 7), N_ROW))
    return tables.reshape(N_ROW * SLOTS, N_COL)


def with_ends(values, key, smallest, high):
    spot = [jax.random.randint(jax.random.fold_in(key, axis), (), 0, length) for axis, length in enumerate(values.shape)]
    main_axis = values.shape.index(max(values.shape))
    beside = spot[:main_axis] + [(spot[main_axis] + 1) % values.shape[main_axis]] + spot[main_axis + 1:]
    return values.at[tuple(spot)].set(smallest).at[tuple(beside)].set(high)


def block_scale(rng, dims, shards, least, top_value):
    gain, own = 1.0, jax.random.fold_in(rng, 6)
    for axis_at, blocks in shards:
        heights = jnp.exp(jax.random.uniform(jax.random.fold_in(own, axis_at), (blocks,), jnp.float32, least / len(shards), top_value / len(shards)))
        gain = gain * jnp.repeat(heights, dims[axis_at] // blocks).reshape([-1 if axis == axis_at else 1 for axis in range(len(dims))])
    return gain


def centred(own_key, shape, width, limit, shards=(), kind=jnp.bfloat16):
    result = jax.random.normal(own_key, shape, jnp.float32) * width
    if len(shards) > 0:
        result = block_scale(own_key, shape, shards, -0.22, 0.18) * result
    return jnp.clip(result, min=-limit, max=limit).astype(kind)


def setup_inputs(seed: int = 0) -> dict:
    splits = jax.random.split(jax.random.key(seed), 9)
    return {
        "in_map": centred(splits[0], (H, W, C), 1.0, 6.0, ((0, 8), (1, 4))),
        "tile_w": centred(splits[1], (3, 3, C, C), (9 * C) ** -0.5, 0.125),
        "head_w1": centred(splits[2], (3, 3, C, C), (9 * C) ** -0.5, 0.125),
        "head_w2": centred(splits[3], (3, 3, C, C), (9 * C) ** -0.5, 0.125),
        "box_row": with_ends(jax.random.randint(splits[4], (N_ROW * SLOTS, N_COL), 0, TR - BOX + 1), jax.random.fold_in(splits[4], 1), 0, TR - BOX).astype(jnp.int32),
        "box_col": with_ends(jax.random.randint(splits[5], (N_ROW * SLOTS, N_COL), 0, TC - BOX + 1), jax.random.fold_in(splits[5], 1), 0, TC - BOX).astype(jnp.int32),
        "box_target": draw_box_target(jax.random.fold_in(splits[8], 71), 0),
        "head_cot": centred(splits[7], (N_ROW * HB, N_COL, BOX, BOX, C), 1.0, 6.0, ((0, 8), (1, 4))),
    }


HIGHEST = lax.Precision.HIGHEST
LAYOUT = ('NHWC', 'HWIO', 'NHWC')

def conv_same(inputs, kernel):
    return lax.conv_general_dilated(inputs.astype(jnp.float32), kernel.astype(jnp.float32), (1, 1), ((1, 1), (1, 1)), dimension_numbers=LAYOUT, precision=HIGHEST)

def flip_weights(kernel):
    return jnp.transpose(jnp.flip(kernel, (0, 1)), (0, 1, 3, 2))

def silu_slope(values):
    sigma = jax.nn.sigmoid(values)
    return sigma * (1.0 + values * (1.0 - sigma))

def weight_grad(inputs, deltas):
    channels = inputs.shape[-1]
    box_side = inputs.shape[1]
    padded = jnp.pad(inputs.astype(jnp.float32), ((0, 0), (1, 1), (1, 1), (0, 0)))
    flat_delta = deltas.astype(jnp.float32).reshape(-1, channels)
    blocks = []
    for shift_y in range(3):
        for shift_x in range(3):
            window = padded[:, shift_y:shift_y + box_side, shift_x:shift_x + box_side, :].reshape(-1, channels)
            blocks.append(jnp.dot(window.T, flat_delta, precision=HIGHEST))
    return jnp.stack(blocks).reshape(3, 3, channels, channels)

def reference(in_map, tile_w, head_w1, head_w2, box_row, box_col, box_target, head_cot):
    preact = conv_same(in_map[None], tile_w)[0]
    feature = jax.nn.silu(preact).astype(jnp.bfloat16)
    flat_target = box_target.reshape(N_ROW, SLOTS * N_COL)
    wanted = jnp.arange(N_COL * HB, dtype=jnp.int32)
    positions = jnp.arange(SLOTS * N_COL, dtype=jnp.int32)
    matches = flat_target[:, None, :] == wanted[None, :, None]
    source = lax.optimization_barrier(jnp.sum(jnp.where(matches, positions[None, None, :], 0), axis=2)).astype(jnp.int32)
    local_y = jnp.take_along_axis(box_row.reshape(N_ROW, SLOTS * N_COL), source, axis=1)
    local_x = jnp.take_along_axis(box_col.reshape(N_ROW, SLOTS * N_COL), source, axis=1)
    anchor_y = (jnp.arange(N_ROW, dtype=jnp.int32)[:, None] * TR + local_y).reshape(-1).astype(jnp.int32)
    anchor_x = (source % N_COL * TC + local_x).reshape(-1).astype(jnp.int32)
    zero_index = jnp.zeros((), jnp.int32)
    crops = jax.vmap(lambda y, x: lax.dynamic_slice(feature, (y, x, zero_index), (BOX, BOX, C)))(anchor_y, anchor_x)
    cotangent = head_cot.reshape(N_ROW, HB, N_COL, BOX, BOX, C).transpose(0, 2, 1, 3, 4, 5).reshape(-1, BOX, BOX, C)
    pre_one = conv_same(crops, head_w1)
    hidden = jax.nn.silu(pre_one).astype(jnp.bfloat16)
    pre_two = conv_same(hidden, head_w2)
    delta_two = (cotangent.astype(jnp.float32) * silu_slope(pre_two)).astype(jnp.bfloat16)
    delta_one = (conv_same(delta_two, flip_weights(head_w2)) * silu_slope(pre_one)).astype(jnp.bfloat16)
    box_grads = conv_same(delta_one, flip_weights(head_w1)).astype(jnp.bfloat16)
    factor = 1.0 / math.sqrt(N_ROW * N_COL * HB * BOX * BOX)
    grad_w1 = weight_grad(crops, delta_one) * factor
    grad_w2 = weight_grad(hidden, delta_two) * factor
    offsets = jnp.arange(BOX, dtype=jnp.int32)
    row_index = anchor_y[:, None, None] + offsets[None, :, None]
    col_index = anchor_x[:, None, None] + offsets[None, None, :]
    box_total = jnp.zeros((N_ROW * TR, N_COL * TC, C), jnp.float32).at[row_index, col_index].add(box_grads.astype(jnp.float32))
    delta_map = (box_total * silu_slope(preact)).astype(jnp.bfloat16)
    grad_map = conv_same(delta_map[None], flip_weights(tile_w))[0].astype(jnp.bfloat16)
    return (grad_map, grad_w1, grad_w2)
```

```python
import functools
import math

import jax
import jax.numpy as jnp
from jax import lax
from jax.experimental import pallas as pl
from jax.experimental.pallas import tpu as pltpu
from jax.sharding import PartitionSpec as P

LAYOUT = ("NHWC", "HWIO", "NHWC")
F32 = jnp.float32
BF16 = jnp.bfloat16
PITCH = 16


def flip_weights(kernel):
    return jnp.transpose(jnp.flip(kernel, (0, 1)), (0, 1, 3, 2))


def conv_valid(inputs, kernel):
    return lax.conv_general_dilated(
        inputs[None],
        kernel,
        (1, 1),
        ((0, 0), (0, 0)),
        dimension_numbers=LAYOUT,
        preferred_element_type=F32,
    )[0]


def slope_of(values):
    sigma = jax.nn.sigmoid(values)
    return sigma * (1.0 + values * (1.0 - sigma))


def shift_rim(shard, axis, dim):
    size, length = lax.axis_size(axis), shard.shape[dim]
    up = [(i, i + 1) for i in range(size - 1)]
    down = [(j, i) for i, j in up]
    before = lax.ppermute(lax.slice_in_dim(shard, length - 1, length, axis=dim), axis, up)
    after = lax.ppermute(lax.slice_in_dim(shard, 0, 1, axis=dim), axis, down)
    return jnp.concatenate([before, shard, after], axis=dim)


def with_rim(shard):
    return shift_rim(shift_rim(shard, "col", 1), "row", 0)


def swap(values, axis, mask, stride=1):
    size = lax.axis_size(axis)
    return lax.ppermute(values, axis, [(i, i ^ (mask * stride)) for i in range(size)])


def place_in(axis, stride, group):
    return (lax.axis_index(axis) // stride) % group


def scatter_sum(values, axis, stride):
    group = values.shape[0]
    mine = place_in(axis, stride, group)
    own = lax.dynamic_index_in_dim(values, mine, 0, keepdims=False)
    parts = [
        swap(lax.dynamic_index_in_dim(values, mine ^ m, 0, keepdims=False), axis, m, stride)
        for m in range(1, group)
    ]
    total = own.astype(F32)
    for part in parts:
        total = total + part.astype(F32)
    return total.astype(BF16)


def gather_all(piece, axis, stride, group):
    mine = place_in(axis, stride, group)
    parts = [swap(piece, axis, m, stride) for m in range(1, group)]
    whole = jnp.zeros((group,) + piece.shape, piece.dtype)
    whole = lax.dynamic_update_index_in_dim(whole, piece, mine, 0)
    for m, part in enumerate(parts, 1):
        whole = lax.dynamic_update_index_in_dim(whole, part, mine ^ m, 0)
    return whole


def levels_of(row_size, col_size):
    levels = []
    for axis, size, first in (("row", row_size, 2), ("col", col_size, 4)):
        stride, group = 1, first
        while stride < size:
            group = min(group, size // stride)
            levels.append((axis, stride, group))
            stride, group = stride * group, 4
    return levels


def sum_all(partial):
    levels = levels_of(lax.axis_size("row"), lax.axis_size("col"))
    shape = partial.shape
    groups = [group for _, _, group in levels]
    values = partial.reshape(*groups, -1, shape[-1])
    for axis, stride, _ in levels:
        values = scatter_sum(values, axis, stride)
    for axis, stride, group in reversed(levels):
        values = gather_all(values, axis, stride, group)
    return values.reshape(shape)


def vmem():
    return pl.BlockSpec(memory_space=pltpu.VMEM)


def smem():
    return pl.BlockSpec(memory_space=pltpu.SMEM)


def params():
    return pltpu.CompilerParams(vmem_limit_bytes=60 << 20)


def inside(rows, side):
    q = lax.broadcasted_iota(jnp.int32, (rows, 1), 0)
    row = lax.rem(lax.div(q, PITCH), side + 1)
    return (row < side) & (lax.rem(q, PITCH) < side)


def store_shifted(ref, start, values, channels, back):
    rows = values.shape[0]
    one = 1 if back else rows - 1
    ref[pl.ds(start, rows), 0:channels] = pltpu.roll(values, one, 0).astype(BF16)
    ref[pl.ds(start, rows), channels : 2 * channels] = values.astype(BF16)
    ref[pl.ds(start, rows), 2 * channels :] = pltpu.roll(values, rows - one, 0).astype(BF16)


def clear_ends(ref, start, rows):
    zero = jnp.zeros((PITCH, ref.shape[1]), BF16)
    ref[0:PITCH, :] = zero
    ref[start + rows : start + rows + PITCH, :] = zero


def conv_rows(ref, start, rows, weight):
    cols = jnp.concatenate(
        [ref[pl.ds(pl.multiple_of(start + a * PITCH - PITCH, PITCH), rows), :] for a in range(3)],
        axis=1,
    )
    return jnp.dot(cols, weight[...], preferred_element_type=F32)


def pick_kernel(head_ref, cot_ref, *out_refs):
    n = 0
    for out in out_refs:
        for k in range(out.shape[0]):
            out[k] = cot_ref[head_ref[n]]
            n += 1


def forward_kernel(
    side, width, anchor_ref, feature_ref, w1_ref, w2_ref,
    crop_t_ref, hidden_t_ref, slope1_ref, slope2_ref, place_ref, frame_ref, frame2_ref,
):
    cells, channels = feature_ref.shape
    boxes = anchor_ref.shape[0]
    frame = (side + 1) * PITCH
    step = 2 * frame
    total = boxes * frame
    q = lax.broadcasted_iota(jnp.int32, (frame, cells), 0)
    n = lax.broadcasted_iota(jnp.int32, (frame, cells), 1)
    row, col = lax.div(q, PITCH), lax.rem(q, PITCH)
    place_ref[...] = jnp.where((row < side) & (col < side), n - row * width - col, -1)
    clear_ends(frame_ref, PITCH, total)
    clear_ends(frame2_ref, PITCH, total)
    feature = feature_ref[...]

    def crop(p, carry):
        hot = jnp.where(place_ref[...] == anchor_ref[p], 1.0, 0.0).astype(BF16)
        values = jnp.dot(hot, feature, preferred_element_type=F32)
        start = pl.multiple_of(PITCH + p * frame, PITCH)
        store_shifted(frame_ref, start, values, channels, True)
        return carry

    lax.fori_loop(0, boxes, crop, 0)
    mask = inside(step, side)

    def one(i, carry):
        at = pl.multiple_of(i * step, PITCH)
        pre = conv_rows(frame_ref, PITCH + at, step, w1_ref)
        sigma = jax.nn.sigmoid(pre)
        slope1_ref[pl.ds(at, step), :] = sigma * (1.0 + pre * (1.0 - sigma))
        store_shifted(
            frame2_ref, pl.multiple_of(PITCH + at, PITCH), jnp.where(mask, pre * sigma, 0.0), channels, True
        )
        return carry

    lax.fori_loop(0, boxes // 2, one, 0)

    def two(i, carry):
        at = pl.multiple_of(i * step, PITCH)
        slope2_ref[pl.ds(at, step), :] = slope_of(conv_rows(frame2_ref, PITCH + at, step, w2_ref))
        return carry

    lax.fori_loop(0, boxes // 2, two, 0)
    for source, out in ((frame_ref, crop_t_ref), (frame2_ref, hidden_t_ref)):
        out[...] = source[PITCH : PITCH + total, channels : 2 * channels].T


def weight_sums(values_t_ref, frame_ref, out_ref):
    channels, total = values_t_ref.shape
    for a in range(3):
        rows = frame_ref[(2 - a) * PITCH : (2 - a) * PITCH + total, :]
        sums = jnp.dot(values_t_ref[...], rows, preferred_element_type=F32)
        for b in range(3):
            out_ref[a, b] = sums[:, b * channels : (b + 1) * channels].astype(BF16)


def second_kernel(side, valid_ref, slope_ref, hidden_t_ref, *refs):
    cots, (grad_ref, frame_ref, pad_ref) = refs[:-3], refs[-3:]
    total, channels = slope_ref.shape
    frame = (side + 1) * PITCH
    clear_ends(frame_ref, PITCH, total)
    pad_ref[...] = jnp.zeros_like(pad_ref)
    n = 0
    for cot in cots:
        for k in range(cot.shape[0]):
            pad_ref[0:side, 0:side, :] = cot[k]
            at = n * frame
            value = pad_ref[...].reshape(frame, channels).astype(F32)
            value = jnp.where(valid_ref[n] > 0, value * slope_ref[at : at + frame, :], 0.0)
            store_shifted(frame_ref, PITCH + at, value, channels, False)
            n += 1
    weight_sums(hidden_t_ref, frame_ref, grad_ref)


def first_kernel(side, slope_ref, crop_t_ref, weight_ref, frame2_ref, grad_ref, frame_ref):
    total, channels = slope_ref.shape
    step = 2 * (side + 1) * PITCH
    clear_ends(frame_ref, PITCH, total)
    mask = inside(step, side)

    def back(i, carry):
        at = pl.multiple_of(i * step, PITCH)
        value = conv_rows(frame2_ref, PITCH + at, step, weight_ref) * slope_ref[pl.ds(at, step), :]
        store_shifted(
            frame_ref, pl.multiple_of(PITCH + at, PITCH), jnp.where(mask, value, 0.0), channels, False
        )
        return carry

    lax.fori_loop(0, total // step, back, 0)
    weight_sums(crop_t_ref, frame_ref, grad_ref)


def map_kernel(side, cell_ref, slope_ref, weight_ref, frame_ref, out_ref, grads_ref):
    total = cell_ref.shape[1]
    cells, channels = out_ref.shape
    step = 2 * (side + 1) * PITCH

    def back(i, carry):
        at = pl.multiple_of(i * step, PITCH)
        grads_ref[pl.ds(at, step), :] = conv_rows(frame_ref, PITCH + at, step, weight_ref).astype(BF16)
        return carry

    lax.fori_loop(0, total // step, back, 0)
    n = lax.broadcasted_iota(jnp.int32, (cells, total), 0)
    hot = jnp.where(n == cell_ref[...], 1.0, 0.0).astype(BF16)
    sums = jnp.dot(hot, grads_ref[...], preferred_element_type=F32)
    out_ref[...] = (sums * slope_ref[...]).astype(BF16)


def ranks(match):
    ids = jnp.arange(match.shape[-1], dtype=jnp.int32)
    before = ids[None, :] < ids[:, None]
    return jnp.sum((match[..., None, :] & before).astype(jnp.int32), axis=-1)


def body(in_map, tile_w, head_w1, head_w2, box_row, box_col, box_target, head_cot):
    tile_rows, tile_cols, channels = in_map.shape
    heads, side = head_cot.shape[0], head_cot.shape[2]
    slots = box_target.shape[0]
    columns = lax.axis_size("col")
    capacity = slots // columns
    me = lax.axis_index("col")
    shape = jax.ShapeDtypeStruct
    frame = (side + 1) * PITCH
    total = slots * frame
    cells = tile_rows * tile_cols
    places = jnp.arange(capacity, dtype=jnp.int32)
    masks = jnp.arange(columns, dtype=jnp.int32)

    target = box_target[:, 0]
    tables = jnp.stack([target] + [swap(target, "col", m) for m in range(1, columns)])
    wanted = (tables >= 0) & (tables // heads == me)
    hot = wanted[:, None, :] & (ranks(wanted)[:, None, :] == places[None, :, None])
    chosen = jnp.sum(jnp.where(hot, (tables % heads)[:, None, :], 0), axis=2).reshape(-1)
    sends = pl.pallas_call(
        pick_kernel,
        out_shape=[shape((capacity,) + head_cot.shape[2:], BF16)] * columns,
        in_specs=[smem(), vmem()],
        out_specs=[vmem()] * columns,
        compiler_params=params(),
        name="pick",
    )(chosen, head_cot[:, 0])
    cots = [sends[0]] + [swap(sends[m], "col", m) for m in range(1, columns)]

    mine = (target >= 0)[None, :] & ((target // heads)[None, :] == (me ^ masks)[:, None])
    hot = mine[:, None, :] & (ranks(mine)[:, None, :] == places[None, :, None])
    corner = box_row[:, 0] * tile_cols + box_col[:, 0]
    anchor = jnp.sum(jnp.where(hot, corner[None, None, :], 0), axis=2).reshape(-1)
    valid = jnp.sum(hot.astype(jnp.int32), axis=2).reshape(-1)
    q = jnp.arange(frame, dtype=jnp.int32)
    row, col = q // PITCH, q % PITCH
    real = (row < side) & (col < side)
    cell = jnp.where(real[None, :], anchor[:, None] + (row * tile_cols + col)[None, :], -1)
    cell = cell.reshape(1, total)

    preact = conv_valid(with_rim(in_map), tile_w).reshape(cells, channels)
    feature = jax.nn.silu(preact).astype(BF16)
    map_slope = slope_of(preact)

    w1 = head_w1.reshape(-1, channels)
    w2 = head_w2.reshape(-1, channels)
    back1, back2 = (
        jnp.transpose(jnp.flip(w, (0,)), (0, 1, 3, 2)).reshape(-1, channels) for w in (head_w1, head_w2)
    )
    frames = shape((total + 2 * PITCH, 3 * channels), BF16)
    grads = shape(head_w1.shape, BF16)
    rows32 = shape((total, channels), F32)
    flops = 2 * total * 9 * channels * channels

    crop_t, hidden_t, slope1, slope2 = pl.pallas_call(
        functools.partial(forward_kernel, side, tile_cols),
        out_shape=[shape((channels, total), BF16)] * 2 + [rows32] * 2,
        in_specs=[smem()] + [vmem()] * 3,
        out_specs=[vmem()] * 4,
        scratch_shapes=[
            pltpu.VMEM((frame, cells), jnp.int32),
            pltpu.VMEM(frames.shape, BF16),
            pltpu.VMEM(frames.shape, BF16),
        ],
        compiler_params=params(),
        cost_estimate=pl.CostEstimate(flops=2 * flops, bytes_accessed=8 << 20, transcendentals=0),
        name="forward",
    )(anchor, feature, w1, w2)

    grad2, frame2 = pl.pallas_call(
        functools.partial(second_kernel, side),
        out_shape=[grads, frames],
        in_specs=[smem()] + [vmem()] * (2 + columns),
        out_specs=[vmem()] * 2,
        scratch_shapes=[pltpu.VMEM((side + 1, PITCH, channels), BF16)],
        compiler_params=params(),
        cost_estimate=pl.CostEstimate(flops=flops, bytes_accessed=8 << 20, transcendentals=0),
        name="second",
    )(valid, slope2, hidden_t, *cots)
    sum2 = sum_all(grad2)

    grad1, frame1 = pl.pallas_call(
        functools.partial(first_kernel, side),
        out_shape=[grads, frames],
        in_specs=[vmem()] * 4,
        out_specs=[vmem()] * 2,
        compiler_params=params(),
        cost_estimate=pl.CostEstimate(flops=2 * flops, bytes_accessed=8 << 20, transcendentals=0),
        name="first",
    )(slope1, crop_t, back2, frame2)
    sum1 = sum_all(grad1)

    delta_map = pl.pallas_call(
        functools.partial(map_kernel, side),
        out_shape=shape((cells, channels), BF16),
        in_specs=[vmem()] * 4,
        out_specs=vmem(),
        scratch_shapes=[pltpu.VMEM((total, channels), BF16)],
        compiler_params=params(),
        cost_estimate=pl.CostEstimate(flops=flops, bytes_accessed=8 << 20, transcendentals=0),
        name="boxes",
    )(cell, map_slope, back1, frame1)
    delta_rim = with_rim(delta_map.reshape(tile_rows, tile_cols, channels))
    grad_map = conv_valid(delta_rim, flip_weights(tile_w)).astype(BF16)

    factor = 1.0 / math.sqrt(lax.axis_size("row") * columns * heads * side * side)
    return (grad_map, sum1.astype(F32) * factor, sum2.astype(F32) * factor)


def solution(mesh):
    in_specs = (
        P("row", "col", None),
        P(),
        P(),
        P(),
        P("row", "col"),
        P("row", "col"),
        P("row", "col"),
        P("row", "col", None, None, None),
    )
    out_specs = (P("row", "col", None), P(), P())
    return jax.shard_map(body, mesh=mesh, in_specs=in_specs, out_specs=out_specs, check_vma=False)
```
